32 devices in a mesh: grp: 2 (over y), pool: 4 (over z), head: 2 (over x), aux: 2 (over core).
Axes of the slice: x: 2, y: 2, z: 4, core: 2. Of those that a mesh axis runs over, the one named last changes fastest.
Arguments:
- hidden: bfloat16 [16, 8192], P('grp', ('pool', 'head', 'aux')), parts along dimension 0, may hold values from -0.59765625 to 0.59765625
- gain: float32 [8192], P(('pool', 'head', 'aux')), may hold values from 0.5 to 1.5
- queries: bfloat16 [16, 8192], P(('grp', 'pool'), 'aux'), parts along dimension 0, may hold values from -6 to 6
- new_key: bfloat16 [16, 1024], P(('grp', 'pool'), 'aux'), parts along dimension 0, may hold values from -6 to 6
- new_value: bfloat16 [16, 1024], P(('grp', 'pool'), 'aux'), parts along dimension 0, may hold values from -6 to 6
- cache_key: bfloat16 [16, 512, 1024], P(('grp', 'pool'), 'head', 'aux'), parts along dimension 0, may hold values from -6 to 6
- cache_value: bfloat16 [16, 512, 1024], P(('grp', 'pool'), 'head', 'aux'), parts along dimension 0, may hold values from -6 to 6
- lengths: int32 [16], P('grp'), parts along dimension 0, may hold values from 170 to 512, as said below
- slot_of: int32 [16], P('grp'), parts along dimension 0, may hold values from 0 to 7, as said below
- out_proj: bfloat16 [2, 4096, 8192], P('aux', 'head', 'pool'), may hold values from -0.09375 to 0.09375
- lm_head: bfloat16 [8192, 65536], P(None, ('pool', 'head', 'aux')), may hold values from -1 to 1
Outputs:
- logits: float32 [16, 65536], P('grp', ('pool', 'head', 'aux')), parts along dimension 0
- entropy: float32 [16], P('grp'), parts along dimension 0
The draws below stay inside these ranges and needn't reach their ends.
There are 2 independent parts, one for each index of `grp`. The reference program is written for one: setup_inputs(seed, part) draws one part's arguments, and reference() takes and returns one part's arrays. A program takes and returns all parts, laid end to end along the dimension named above; an argument that names none is the same for every part. Nothing has to cross between parts.
Inputs may be any that keep to these rules, and one draw needn't show every extreme that they name: `lengths`: some request fills all 512 positions and some has exactly 170. `slot_of`: each slot holds exactly one request; the requests of one index of pool have their slots together on one index of pool.
All inputs are finite; a program needn't handle non-finite values.
Results may differ from the reference program's by a relative error of at most 0.02.
Values may be sent and summed in bfloat16 or wider, within the bound.
No kernel may reach another device: no remote copies, remote signals or barrier semaphores. Data moves between devices by JAX's collectives and lax.ppermute only.
A program may use at most 128 MiB of HBM per device.

```python
import math
import jax
import jax.numpy as jnp
from jax import lax

D = 8192
QH = 64
KVH = 8
HD = 128
VOCAB = 65536
REQ_DEV = 2
CAP = 512
REQS = 8
N_POOL = 4
N_AUX = 2


def draw_lengths(key, part):
    lowest = CAP // 3
    base = jax.random.randint(jax.random.fold_in(key, 11), (REQS,), lowest, CAP + 1)
    first = jax.random.randint(jax.random.fold_in(key, 12), (), 0, REQS)
    offset = jax.random.randint(jax.random.fold_in(key, 13), (), 1, REQS)
    second = (first + offset) % REQS
    places = jnp.arange(REQS, dtype=jnp.int32)
    base = jnp.where(places == first, CAP, base)
    base = jnp.where(places == second, lowest, base)
    return base.astype(jnp.int32)


def draw_slot_of(key, part):
    count = N_POOL
    if count >= 4:
        cycle = [0, 1, 1 + count // 2, count // 2]
    elif count >= 2:
        cycle = [0, 1]
    else:
        cycle = [0]
    targets = cycle[1:] + cycle[:1]
    others = [place for place in range(count) if place not in cycle]
    mapping = jnp.zeros((count,), jnp.int32)
    mapping = mapping.at[jnp.array(cycle, dtype=jnp.int32)].set(jnp.array(targets, dtype=jnp.int32))
    if len(others) > 0:
        rest = jnp.array(others, dtype=jnp.int32)
        mixing = jax.random.permutation(jax.random.fold_in(key, 31), len(others))
        mapping = mapping.at[rest].set(rest[mixing])
    rotate = jax.random.randint(jax.random.fold_in(key, 32), (), 0, count)
    inner = jax.random.randint(jax.random.fold_in(key, 33), (count,), 0, REQ_DEV)
    request = jnp.arange(REQS, dtype=jnp.int32)
    home = request // REQ_DEV
    target = (mapping[(home - rotate) % count] + rotate) % count
    within = (request % REQ_DEV + inner[home]) % REQ_DEV
    return (target * REQ_DEV + within).astype(jnp.int32)


def draw_lm_head(key, part):
    column = jnp.arange(VOCAB, dtype=jnp.float32) / (VOCAB - 1)
    rise = 1.0 + column
    jitter = jnp.exp(jax.random.uniform(jax.random.fold_in(key, 21), (VOCAB,), minval=0.0, maxval=math.log(2.0)))
    entries = jax.random.truncated_normal(jax.random.fold_in(key, 22), -4.0, 4.0, (D, VOCAB))
    scaled = entries * (rise * jitter)[None, :] / math.sqrt(D)
    scaled = jnp.clip(scaled, -1.0, 1.0)
    return scaled.astype(jnp.bfloat16)


def with_spikes(drawn, rng, source, target, blocks, factor):
    def block_of(axis_at):
        return (jnp.arange(drawn.shape[axis_at]) // (drawn.shape[axis_at] // blocks)).reshape((-1,) + (1,) * (drawn.ndim - 1 - axis_at))

    first = jax.random.permutation(rng, blocks)[block_of(target)]
    other_side = (block_of(target) + blocks // 2) % blocks
    return jnp.where((block_of(source) == first) | (block_of(source) == other_side), factor * drawn, drawn)


def block_levels(own_key, dims, pieces, low, top_value):
    def one(dim, parts):
        steps = jax.random.uniform(jax.random.fold_in(jax.random.fold_in(own_key, 6), dim), (parts,), jnp.float32, low / len(pieces), top_value / len(pieces))
        return jnp.repeat(jnp.exp(steps), dims[dim] // parts).reshape((-1,) + (1,) * (len(dims) - dim - 1))

    level = one(*pieces[0])
    for cut in pieces[1:]:
        level = level * one(*cut)
    return level


def bell_draw(own_key, shape, deviation, bound, pieces=(), kind=jnp.bfloat16):
    drawn = jax.random.normal(own_key, shape, jnp.float32) * deviation
    if len(pieces) > 0:
        drawn = block_levels(own_key, shape, pieces, -0.22, 0.18) * drawn
    return jnp.clip(drawn, min=-bound, max=bound).astype(kind)


def heavy_noise(key, dims, scale, reach, cuts, heavy, held_as=jnp.bfloat16):
    result = scale * jax.random.normal(key, dims, jnp.float32)
    if cuts:
        result = result * block_levels(key, dims, cuts, -0.22, 0.18)
    return jnp.clip(with_spikes(result, jax.random.fold_in(key, 3), *heavy), -reach, reach).astype(held_as)


def setup_inputs(seed: int = 0, part: int = 0) -> dict:
    splits = jax.random.split(jax.random.key(seed), 12)
    part_splits = jax.random.split(jax.random.fold_in(splits[11], part), 12)
    hidden = bell_draw(part_splits[0], (REQS, D), 0.1, 0.59765625, ((1, 16),))
    gain = jnp.clip(1.0 + 0.1 * jax.random.normal(splits[1], (D,), jnp.float32), 0.5, 1.5)
    queries = bell_draw(part_splits[2], (REQS, QH * HD), 1.0, 6.0, ((0, 4), (1, 2)))
    new_key = bell_draw(part_splits[3], (REQS, KVH * HD), 1.0, 6.0, ((0, 4), (1, 2)))
    new_value = bell_draw(part_splits[4], (REQS, KVH * HD), 1.0, 6.0, ((0, 4), (1, 2)))
    cache_key = bell_draw(part_splits[5], (REQS, CAP, KVH * HD), 1.0, 6.0, ((0, 4), (1, 2), (2, 2)))
    cache_value = bell_draw(part_splits[6], (REQS, CAP, KVH * HD), 1.0, 6.0, ((0, 4), (1, 2), (2, 2)))
    lengths = draw_lengths(jax.random.fold_in(jax.random.fold_in(splits[11], part), 71), part)
    slot_of = draw_slot_of(jax.random.fold_in(jax.random.fold_in(splits[11], part), 71), part)
    out_proj = heavy_noise(splits[9], (N_AUX, QH * HD // N_AUX, D), (QH * HD) ** -0.5, 0.09375, ((0, 2), (1, 2), (2, 4)), (1, 2, 4, 2.0))
    lm_head = draw_lm_head(jax.random.fold_in(splits[11], 71), part)
    return dict(hidden=hidden, gain=gain, queries=queries, new_key=new_key, new_value=new_value, cache_key=cache_key, cache_value=cache_value, lengths=lengths, slot_of=slot_of, out_proj=out_proj, lm_head=lm_head)


def reference(hidden, gain, queries, new_key, new_value, cache_key, cache_value, lengths, slot_of, out_proj, lm_head):
    group = QH // KVH
    scale = 1.0 / math.sqrt(HD)
    keys = jnp.take(cache_key, slot_of, axis=0).reshape(REQS, CAP, KVH, HD).astype(jnp.float32)
    values = jnp.take(cache_value, slot_of, axis=0).reshape(REQS, CAP, KVH, HD).astype(jnp.float32)
    query_heads = queries.reshape(REQS, KVH, group, HD).astype(jnp.float32)
    scores = jnp.einsum('rkgd,rtkd->rkgt', query_heads, keys, precision=lax.Precision.HIGHEST) * scale
    position = jnp.arange(CAP, dtype=jnp.int32)
    live = position[None, :] < lengths[:, None]
    weights = jnp.where(live[:, None, None, :], jnp.exp(scores), 0.0)
    rounded = lax.optimization_barrier(weights.astype(jnp.bfloat16)).astype(jnp.float32)
    own_keys = new_key.reshape(REQS, KVH, 1, HD).astype(jnp.float32)
    own_values = new_value.reshape(REQS, KVH, 1, HD).astype(jnp.float32)
    own = jnp.exp(lax.optimization_barrier(jnp.sum(query_heads * own_keys, axis=3)) * scale)
    total = lax.optimization_barrier(jnp.sum(weights, axis=3)) + own
    mixed = jnp.einsum('rkgt,rtkd->rkgd', rounded, values, precision=lax.Precision.HIGHEST)
    mixed = mixed + own[..., None] * own_values
    attended = (mixed / total[..., None]).astype(jnp.bfloat16).reshape(REQS, QH * HD)
    projected = jnp.dot(attended, out_proj.reshape(QH * HD, D), preferred_element_type=jnp.float32)
    stream = (hidden.astype(jnp.float32) + projected).astype(jnp.bfloat16)
    stream = lax.optimization_barrier(stream).astype(jnp.float32)
    mean_sq = lax.optimization_barrier(jnp.mean(stream * stream, axis=1, keepdims=True))
    normed = (stream * lax.rsqrt(mean_sq + 1e-05) * gain[None, :]).astype(jnp.bfloat16)
    logits = jnp.dot(normed, lm_head, preferred_element_type=jnp.float32)
    expd = jnp.exp(logits)
    vocab_total = lax.optimization_barrier(jnp.sum(expd, axis=1))
    moment = lax.optimization_barrier(jnp.sum(expd * logits, axis=1))
    entropy = jnp.log(vocab_total) - moment / vocab_total
    return (logits, entropy)
```

```python
import math

import jax
import jax.numpy as jnp
from jax import lax
from jax.sharding import PartitionSpec as P

HD = 128


def swap(x, axis, size, step):
    return lax.ppermute(x, axis, [(i, i ^ step) for i in range(size)])


def gather(x, axis, size, dim):
    place = lax.axis_index(axis)
    step = 1
    while step < size:
        y = swap(x, axis, size, step)
        upper = (place & step) != 0
        x = jnp.concatenate([jnp.where(upper, y, x), jnp.where(upper, x, y)], dim)
        step *= 2
    return x


def total_over(x, axes_sizes):
    for axis, size in axes_sizes:
        step = 1
        while step < size:
            x = x + swap(x, axis, size, step)
            step *= 2
    return x


def make_per_device(sizes):
    n_pool, n_head, n_aux = sizes["pool"], sizes["head"], sizes["aux"]

    def per_device(
        hidden,
        gain,
        queries,
        new_key,
        new_value,
        cache_key,
        cache_value,
        lengths,
        slot_of,
        out_proj,
        lm_head,
    ):
        f32, bf16 = jnp.float32, jnp.bfloat16
        slots_here, span = cache_key.shape[0], cache_key.shape[1]
        kv_here = cache_key.shape[2] // HD
        q_here = queries.shape[1] // HD
        group = q_here // kv_here
        requests = hidden.shape[0]
        scale = 1.0 / math.sqrt(HD)
        pool_place = lax.axis_index("pool")
        head_place = lax.axis_index("head")
        aux_place = lax.axis_index("aux")

        gain_rows = gain.astype(bf16).reshape(slots_here, -1)
        mine = jnp.concatenate([queries, new_key, new_value, gain_rows], 1)
        every = gather(mine, "pool", n_pool, 0)
        nq, nk = queries.shape[1], new_key.shape[1]
        gains = every[:, nq + 2 * nk :]

        slot_ids = pool_place * slots_here + jnp.arange(slots_here, dtype=jnp.int32)
        chosen = slot_of[None, :] == slot_ids[:, None]
        picked = jnp.dot(
            chosen.astype(bf16), every[:, : nq + 2 * nk], preferred_element_type=f32
        ).astype(bf16)
        query_heads = picked[:, :nq].reshape(slots_here, kv_here, group, HD)
        key_own = picked[:, nq : nq + nk].reshape(slots_here, kv_here, 1, HD).astype(f32)
        value_own = picked[:, nq + nk :].reshape(slots_here, kv_here, 1, HD).astype(f32)
        length_slot = jnp.sum(jnp.where(chosen, lengths[None, :], 0), axis=1)
        keys = cache_key.reshape(slots_here, span, kv_here, HD)
        values = cache_value.reshape(slots_here, span, kv_here, HD)
        scores = jnp.einsum("skgd,stkd->skgt", query_heads, keys, preferred_element_type=f32) * scale
        position = head_place * span + jnp.arange(span, dtype=jnp.int32)
        live = position[None, :] < length_slot[:, None]
        weights = jnp.where(live[:, None, None, :], jnp.exp(scores), 0.0)
        own = jnp.exp(jnp.sum(query_heads.astype(f32) * key_own, axis=3) * scale)
        own = jnp.where(head_place == 0, own, 0.0)
        total = jnp.sum(weights, axis=3) + own
        mixed = jnp.einsum("skgt,stkd->skgd", weights.astype(bf16), values, preferred_element_type=f32)
        mixed = (mixed + own[..., None] * value_own).reshape(slots_here, q_here, HD)
        total = total.reshape(slots_here, q_here)

        step = n_head // 2
        while step:
            upper = (head_place & step) != 0
            half = total.shape[1] // 2
            keep_mix = jnp.where(upper, mixed[:, half:], mixed[:, :half])
            send_mix = jnp.where(upper, mixed[:, :half], mixed[:, half:])
            keep_tot = jnp.where(upper, total[:, half:], total[:, :half])
            send_tot = jnp.where(upper, total[:, :half], total[:, half:])
            tot_hi = send_tot.astype(bf16)
            tot_lo = (send_tot - tot_hi.astype(f32)).astype(bf16)
            flat = half * HD
            sent = jnp.concatenate(
                [
                    send_mix.astype(bf16).reshape(slots_here, flat),
                    tot_hi,
                    tot_lo,
                    gains.reshape(slots_here, -1),
                ],
                1,
            )
            came = swap(sent, "head", n_head, step)
            mixed = keep_mix + came[:, :flat].reshape(slots_here, half, HD).astype(f32)
            total = keep_tot + came[:, flat : flat + half].astype(f32)
            total = total + came[:, flat + half : flat + 2 * half].astype(f32)
            other = came[:, flat + 2 * half :].reshape(gains.shape)
            gains = jnp.concatenate(
                [jnp.where(upper, other, gains), jnp.where(upper, gains, other)], 0
            ).reshape(2 * gains.shape[0], -1)
            step //= 2
        attended = (mixed / total[:, :, None]).astype(bf16).reshape(slots_here, -1)
        outputs = gather(attended, "pool", n_pool, 0)
        order = slot_of[:, None] == jnp.arange(requests, dtype=jnp.int32)[None, :]
        by_request = jnp.dot(order.astype(bf16), outputs, preferred_element_type=f32).astype(bf16)

        term = jnp.dot(by_request, out_proj[0], preferred_element_type=f32)
        chunk = hidden.shape[1]
        chunks = n_head * n_aux
        owner = lax.broadcasted_iota(jnp.int32, (1, chunks, 1), 1) == head_place * n_aux + aux_place
        term = term.reshape(requests, chunks, chunk)
        term = term + jnp.where(owner, hidden.astype(f32)[:, None, :], 0.0)
        term = term.reshape(requests, chunks * chunk)
        step = 1
        while step < n_aux:
            upper = (aux_place & step) != 0
            rows = gains.reshape(requests, -1)
            came = swap(jnp.concatenate([term.astype(bf16), rows], 1), "aux", n_aux, step)
            width = term.shape[1]
            term = term + came[:, :width].astype(f32)
            other = came[:, width:].reshape(gains.shape)
            gains = jnp.concatenate(
                [jnp.where(upper, other, gains), jnp.where(upper, gains, other)], 0
            )
            step *= 2
        step = 1
        while step < n_head:
            term = term + swap(term.astype(bf16), "head", n_head, step).astype(f32)
            step *= 2
        stream = term.astype(bf16)

        bits = n_head.bit_length() - 1
        stored = gains.reshape((n_aux,) + (2,) * bits + (n_pool, chunk))
        turn = (1 + bits,) + tuple(range(bits, 0, -1)) + (0, 2 + bits)
        full_gain = jnp.transpose(stored, turn).reshape(-1).astype(f32)

        full = gather(stream, "pool", n_pool, 1).astype(f32)
        mean_sq = jnp.mean(full * full, axis=1, keepdims=True)
        normed = (full * lax.rsqrt(mean_sq + 1e-05) * full_gain[None, :]).astype(bf16)
        logits = jnp.dot(normed, lm_head, preferred_element_type=f32)
        expd = jnp.exp(logits)
        sums = jnp.stack([jnp.sum(expd, axis=1), jnp.sum(expd * logits, axis=1)])
        sums = total_over(sums, (("aux", n_aux), ("head", n_head), ("pool", n_pool)))
        entropy = jnp.log(sums[0]) - sums[1] / sums[0]
        return (logits, entropy)

    return per_device


def solution(mesh):
    in_specs = (
        P("grp", ("pool", "head", "aux")),
        P(("pool", "head", "aux")),
        P(("grp", "pool"), "aux"),
        P(("grp", "pool"), "aux"),
        P(("grp", "pool"), "aux"),
        P(("grp", "pool"), "head", "aux"),
        P(("grp", "pool"), "head", "aux"),
        P("grp"),
        P("grp"),
        P("aux", "head", "pool"),
        P(None, ("pool", "head", "aux")),
    )
    out_specs = (P("grp", ("pool", "head", "aux")), P("grp"))
    return jax.shard_map(
        make_per_device(dict(mesh.shape)),
        mesh=mesh,
        in_specs=in_specs,
        out_specs=out_specs,
        check_vma=False,
    )
```

```python
import math

import jax
import jax.numpy as jnp
from jax import lax
from jax.experimental import pallas as pl
from jax.experimental.pallas import tpu as pltpu
from jax.sharding import PartitionSpec as P

HD = 128


class Rounds:
    def __init__(self, lm_head):
        self.lm_head = lm_head
        self.resident = []

    def swap(self, x, axis, size, step):
        pairs = [(i, i ^ step) for i in range(size)]
        if axis == "aux" or len(self.resident) == WINDOWS:
            return lax.ppermute(x, axis, pairs)
        at = len(self.resident)
        y = lax.ppermute(x, axis, pairs)
        self.resident.append(fetch(self.lm_head, at))
        return y


def gather(rounds, x, axis, size, dim):
    place = lax.axis_index(axis)
    step = 1
    while step < size:
        y = rounds.swap(x, axis, size, step)
        upper = (place & step) != 0
        x = jnp.concatenate([jnp.where(upper, y, x), jnp.where(upper, x, y)], dim)
        step *= 2
    return x


VM = pl.BlockSpec(memory_space=pltpu.VMEM)
HB = pl.BlockSpec(memory_space=pl.ANY)
MIB = 1 << 20
WINDOWS = 8
PIECES = 16


def fetch(lm_head, piece):
    rows = lm_head.shape[0] // PIECES
    cuts = 4
    part = rows // cuts

    def body(src, dst, sem):
        copies = [
            pltpu.make_async_copy(
                src.at[pl.ds(piece * rows + i * part, part)],
                dst.at[pl.ds(i * part, part)],
                sem.at[i],
            )
            for i in range(cuts)
        ]
        for copy in copies:
            copy.start()
        for copy in copies:
            copy.wait()

    return pl.pallas_call(
        body,
        out_shape=pltpu.VMEM((rows, lm_head.shape[1]), lm_head.dtype),
        in_specs=[HB],
        out_specs=VM,
        scratch_shapes=[pltpu.SemaphoreType.DMA((cuts,))],
        cost_estimate=pl.CostEstimate(
            flops=0, bytes_accessed=rows * lm_head.shape[1] * 2, transcendentals=0
        ),
        compiler_params=pltpu.CompilerParams(vmem_limit_bytes=MIB),
    )(lm_head)


def join(*arrays):
    widths = [a.shape[1] for a in arrays]

    def body(*refs):
        at = 0
        for ref, width in zip(refs[:-1], widths):
            refs[-1][:, at : at + width] = ref[...]
            at += width

    return pl.pallas_call(
        body,
        out_shape=jax.ShapeDtypeStruct((arrays[0].shape[0], sum(widths)), arrays[0].dtype),
        in_specs=[VM] * len(arrays),
        out_specs=VM,
        compiler_params=pltpu.CompilerParams(vmem_limit_bytes=2 * MIB),
        name="join",
    )(*arrays)


def project(outputs, order, weight, hidden, place, gains):
    requests, width = outputs.shape[0], weight.shape[1]
    chunk = hidden.shape[1]
    f32, bf16 = jnp.float32, jnp.bfloat16

    def body(place_ref, out_ref, order_ref, w_ref, hid_ref, gain_ref, term_ref, msg_ref):
        rows = out_ref[...].astype(f32)
        pick = order_ref[...]
        sel = jnp.zeros_like(rows)
        for e in range(requests):
            sel = sel + pick[:, e : e + 1] * rows[e : e + 1, :]
        term = jnp.dot(sel.astype(bf16), w_ref[...], preferred_element_type=f32)
        tiled = jnp.concatenate([hid_ref[...].astype(f32)] * (width // chunk), 1)
        owner = lax.broadcasted_iota(jnp.int32, term.shape, 1) // chunk == place_ref[0]
        term = term + jnp.where(owner, tiled, 0.0)
        term_ref[...] = term
        msg_ref[:, :width] = term.astype(bf16)
        msg_ref[:, width:] = gain_ref[...]

    return pl.pallas_call(
        body,
        out_shape=(
            jax.ShapeDtypeStruct((requests, width), f32),
            jax.ShapeDtypeStruct((requests, width + gains.shape[1]), bf16),
        ),
        in_specs=[pl.BlockSpec(memory_space=pltpu.SMEM)] + [VM] * 5,
        out_specs=(VM, VM),
        cost_estimate=pl.CostEstimate(
            flops=2 * requests * weight.size, bytes_accessed=weight.size * 2, transcendentals=0
        ),
        compiler_params=pltpu.CompilerParams(vmem_limit_bytes=4 * MIB),
        name="project",
    )(place, outputs, order, weight, hidden, gains)


def score(x, resident, lm_head):
    requests, depth = x.shape
    width = lm_head.shape[1]
    held = len(resident)
    rows = depth // PIECES
    start = held * rows
    left = PIECES - held
    slots = min(3, left)
    f32, bf16 = jnp.float32, jnp.bfloat16

    def body(x_ref, *refs):
        kept = refs[:held]
        src, out_ref, sum_ref, buf, sem = refs[held:]

        def copy(i):
            return pltpu.make_async_copy(
                src.at[pl.ds(start + i * rows, rows)], buf.at[i % slots], sem.at[i % slots]
            )

        for i in range(slots):
            copy(i).start()

        def multiply(ref, piece, first=False):
            part = jnp.dot(
                x_ref[:, piece * rows : (piece + 1) * rows], ref[...], preferred_element_type=f32
            )
            out_ref[...] = part if first else out_ref[...] + part

        done = 0
        for i in range(held):
            multiply(kept[i], i, i == 0)
            while done < left and done * held < (i + 1) * left:
                copy(done).wait()
                multiply(buf.at[done % slots], held + done)
                if done + slots < left:
                    copy(done + slots).start()
                done += 1
        logits = out_ref[...]
        expd = jnp.exp(logits)
        total = jnp.sum(expd, axis=1, keepdims=True)
        moment = jnp.sum(expd * logits, axis=1, keepdims=True)
        lane = lax.broadcasted_iota(jnp.int32, (requests, 128), 1)
        sum_ref[...] = jnp.where(lane == 0, total, moment)

    return pl.pallas_call(
        body,
        out_shape=(
            jax.ShapeDtypeStruct((requests, width), f32),
            jax.ShapeDtypeStruct((requests, 128), f32),
        ),
        in_specs=[VM] * (1 + held) + [HB],
        out_specs=(VM, VM),
        scratch_shapes=[
            pltpu.VMEM((slots, rows, width), bf16),
            pltpu.SemaphoreType.DMA((slots,)),
        ],
        cost_estimate=pl.CostEstimate(
            flops=2 * requests * lm_head.size,
            bytes_accessed=left * rows * width * 2,
            transcendentals=requests * width,
        ),
        compiler_params=pltpu.CompilerParams(vmem_limit_bytes=slots * rows * width * 2 + 4 * MIB),
        name="score",
    )(x, *resident, lm_head)


def total_over(rounds, x, axes_sizes):
    for axis, size in axes_sizes:
        step = 1
        while step < size:
            x = x + rounds.swap(x, axis, size, step)
            step *= 2
    return x


def make_per_device(sizes):
    n_pool, n_head, n_aux = sizes["pool"], sizes["head"], sizes["aux"]

    def per_device(
        hidden,
        gain,
        queries,
        new_key,
        new_value,
        cache_key,
        cache_value,
        lengths,
        slot_of,
        out_proj,
        lm_head,
    ):
        f32, bf16 = jnp.float32, jnp.bfloat16
        slots_here, span = cache_key.shape[0], cache_key.shape[1]
        kv_here = cache_key.shape[2] // HD
        q_here = queries.shape[1] // HD
        group = q_here // kv_here
        requests = hidden.shape[0]
        scale = 1.0 / math.sqrt(HD)
        pool_place = lax.axis_index("pool")
        head_place = lax.axis_index("head")
        aux_place = lax.axis_index("aux")

        rounds = Rounds(lm_head)
        every = gather(rounds, join(queries, new_key, new_value), "pool", n_pool, 0)
        nq, nk = queries.shape[1], new_key.shape[1]

        slot_ids = pool_place * slots_here + jnp.arange(slots_here, dtype=jnp.int32)
        chosen = slot_of[None, :] == slot_ids[:, None]
        picked = jnp.dot(
            chosen.astype(bf16), every, preferred_element_type=f32
        ).astype(bf16)
        query_heads = picked[:, :nq].reshape(slots_here, kv_here, group, HD)
        key_own = picked[:, nq : nq + nk].reshape(slots_here, kv_here, 1, HD).astype(f32)
        value_own = picked[:, nq + nk :].reshape(slots_here, kv_here, 1, HD).astype(f32)
        length_slot = jnp.sum(jnp.where(chosen, lengths[None, :], 0), axis=1)
        keys = cache_key.reshape(slots_here, span, kv_here, HD)
        values = cache_value.reshape(slots_here, span, kv_here, HD)
        scores = jnp.einsum("skgd,stkd->skgt", query_heads, keys, preferred_element_type=f32) * scale
        position = head_place * span + jnp.arange(span, dtype=jnp.int32)
        live = position[None, :] < length_slot[:, None]
        weights = jnp.where(live[:, None, None, :], jnp.exp(scores), 0.0)
        own = jnp.exp(jnp.sum(query_heads.astype(f32) * key_own, axis=3) * scale)
        own = jnp.where(head_place == 0, own, 0.0)
        total = jnp.sum(weights, axis=3) + own
        mixed = jnp.einsum("skgt,stkd->skgd", weights.astype(bf16), values, preferred_element_type=f32)
        mixed = (mixed + own[..., None] * value_own).reshape(slots_here, q_here, HD)
        total = total.reshape(slots_here, q_here)

        gains = gain.astype(bf16).reshape(1, -1)
        step = n_head // 2
        while step:
            upper = (head_place & step) != 0
            half = total.shape[1] // 2
            keep_mix = jnp.where(upper, mixed[:, half:], mixed[:, :half])
            send_mix = jnp.where(upper, mixed[:, :half], mixed[:, half:])
            keep_tot = jnp.where(upper, total[:, half:], total[:, :half])
            send_tot = jnp.where(upper, total[:, :half], total[:, half:])
            tot_hi = send_tot.astype(bf16)
            tot_lo = (send_tot - tot_hi.astype(f32)).astype(bf16)
            flat = half * HD
            sent = jnp.concatenate(
                [
                    send_mix.astype(bf16).reshape(slots_here, flat),
                    tot_hi,
                    tot_lo,
                    gains.reshape(slots_here, -1),
                ],
                1,
            )
            came = rounds.swap(sent, "head", n_head, step)
            mixed = keep_mix + came[:, :flat].reshape(slots_here, half, HD).astype(f32)
            total = keep_tot + came[:, flat : flat + half].astype(f32)
            total = total + came[:, flat + half : flat + 2 * half].astype(f32)
            other = came[:, flat + 2 * half :].reshape(gains.shape)
            gains = jnp.concatenate(
                [jnp.where(upper, other, gains), jnp.where(upper, gains, other)], 0
            )
            step //= 2
        attended = (mixed / total[:, :, None]).astype(bf16).reshape(slots_here, -1)
        mine = jnp.concatenate([attended, gains.reshape(slots_here, -1)], 1)
        every = gather(rounds, mine, "pool", n_pool, 0)
        outputs, gains = every[:, : attended.shape[1]], every[:, attended.shape[1] :]
        order = slot_of[:, None] == jnp.arange(requests, dtype=jnp.int32)[None, :]

        chunk = hidden.shape[1]
        place = (head_place * n_aux + aux_place).reshape(1)
        term, message = project(
            outputs, order.astype(f32), out_proj[0], hidden, place, gains
        )
        width = term.shape[1]
        step = 1
        while step < n_aux:
            upper = (aux_place & step) != 0
            came = rounds.swap(message, "aux", n_aux, step)
            term = term + came[:, :width].astype(f32)
            other = came[:, width:]
            gains = jnp.stack([jnp.where(upper, other, gains), jnp.where(upper, gains, other)])
            step *= 2
            if step < n_aux:
                gains = gains.reshape(requests, -1)
                message = jnp.concatenate([term.astype(bf16), gains], 1)
        step = 1
        while step < n_head:
            term = term + rounds.swap(term.astype(bf16), "head", n_head, step).astype(f32)
            step *= 2
        stream = term.astype(bf16)

        bits = n_head.bit_length() - 1
        stored = gains.reshape((n_aux, n_pool) + (2,) * bits + (chunk,))
        turn = (1,) + tuple(range(1 + bits, 1, -1)) + (0, 2 + bits)
        full_gain = jnp.transpose(stored, turn).reshape(-1).astype(f32)

        full = gather(rounds, stream, "pool", n_pool, 1).astype(f32)
        mean_sq = jnp.mean(full * full, axis=1, keepdims=True)
        normed = (full * lax.rsqrt(mean_sq + 1e-05) * full_gain[None, :]).astype(bf16)
        logits, sums = score(normed, rounds.resident, lm_head)
        sums = total_over(rounds, sums, (("aux", n_aux), ("head", n_head), ("pool", n_pool)))
        entropy = jnp.log(sums[:, 0]) - sums[:, 1] / sums[:, 0]
        return (logits, entropy)

    return per_device


def solution(mesh):
    in_specs = (
        P("grp", ("pool", "head", "aux")),
        P(("pool", "head", "aux")),
        P(("grp", "pool"), "aux"),
        P(("grp", "pool"), "aux"),
        P(("grp", "pool"), "aux"),
        P(("grp", "pool"), "head", "aux"),
        P(("grp", "pool"), "head", "aux"),
        P("grp"),
        P("grp"),
        P("aux", "head", "pool"),
        P(None, ("pool", "head", "aux")),
    )
    out_specs = (P("grp", ("pool", "head", "aux")), P("grp"))
    return jax.shard_map(
        make_per_device(dict(mesh.shape)),
        mesh=mesh,
        in_specs=in_specs,
        out_specs=out_specs,
        check_vma=False,
    )
```

```python
import math

import jax
import jax.numpy as jnp
from jax import lax
from jax.experimental import pallas as pl
from jax.experimental.pallas import tpu as pltpu
from jax.sharding import PartitionSpec as P

HD = 128
VM = pl.BlockSpec(memory_space=pltpu.VMEM)
HB = pl.BlockSpec(memory_space=pl.ANY)
MIB = 1 << 20
WINDOWS = 8
PIECES = 16
F32, BF16 = jnp.float32, jnp.bfloat16


def call(body, outs, ins, scratch=(), grant=2 * MIB, cost=None):
    return pl.pallas_call(
        body,
        out_shape=outs,
        in_specs=ins,
        out_specs=jax.tree.map(lambda _: VM, outs),
        scratch_shapes=list(scratch),
        cost_estimate=cost,
        compiler_params=pltpu.CompilerParams(vmem_limit_bytes=grant),
    )


def shaped(shape, dtype):
    return jax.ShapeDtypeStruct(tuple(shape), dtype)


def fetch(lm_head, piece):
    rows = lm_head.shape[0] // PIECES
    cuts = 4
    part = rows // cuts

    def body(src, dst, sem):
        copies = [
            pltpu.make_async_copy(
                src.at[pl.ds(piece * rows + i * part, part)],
                dst.at[pl.ds(i * part, part)],
                sem.at[i],
            )
            for i in range(cuts)
        ]
        for copy in copies:
            copy.start()
        for copy in copies:
            copy.wait()

    size = rows * lm_head.shape[1] * 2
    return call(
        body,
        pltpu.VMEM((rows, lm_head.shape[1]), lm_head.dtype),
        [HB],
        [pltpu.SemaphoreType.DMA((cuts,))],
        MIB,
        pl.CostEstimate(flops=0, bytes_accessed=size, transcendentals=0),
    )(lm_head)


class Rounds:
    def __init__(self, lm_head):
        self.lm_head = lm_head
        self.resident = []

    def swap(self, x, axis, size, step):
        pairs = [(i, i ^ step) for i in range(size)]
        if axis == "aux" or len(self.resident) == WINDOWS:
            return lax.ppermute(x, axis, pairs)
        at = len(self.resident)
        y = lax.ppermute(x, axis, pairs)
        self.resident.append(fetch(self.lm_head, at))
        return y


def steps_of(size):
    return [1 << i for i in range(size.bit_length() - 1)]


def is_upper(axis, step):
    return (lax.axis_index(axis) & step) != 0


def merge(x, y, axis, step, dim):
    size = x.shape[dim]

    def body(x_ref, y_ref, o_ref):
        upper = is_upper(axis, step)
        a, b = x_ref[...], y_ref[...]
        low, high = jnp.where(upper, b, a), jnp.where(upper, a, b)
        if dim == 0:
            o_ref[:size, :] = low
            o_ref[size:, :] = high
        else:
            o_ref[:, :size] = low
            o_ref[:, size:] = high

    shape = list(x.shape)
    shape[dim] *= 2
    return call(body, shaped(shape, x.dtype), [VM, VM])(x, y)


def gather(rounds, x, axis, size, dim):
    for step in steps_of(size):
        x = merge(x, rounds.swap(x, axis, size, step), axis, step, dim)
    return x


def join(*arrays):
    widths = [a.shape[1] for a in arrays]

    def body(*refs):
        out, sem = refs[-2:]
        copies, at = [], 0
        for i, width in enumerate(widths):
            copies.append(pltpu.make_async_copy(refs[i], out.at[:, at : at + width], sem.at[i]))
            at += width
        for copy in copies:
            copy.start()
        for copy in copies:
            copy.wait()

    return call(
        body,
        shaped((arrays[0].shape[0], sum(widths)), arrays[0].dtype),
        [pl.BlockSpec(memory_space=pltpu.HBM)] * len(arrays),
        [pltpu.SemaphoreType.DMA((len(arrays),))],
        MIB,
    )(*arrays)


def to_column(row):
    n = row.shape[1]
    diag = lax.broadcasted_iota(jnp.int32, (n, n), 0) == lax.broadcasted_iota(jnp.int32, (n, n), 1)
    return jnp.sum(jnp.where(diag, jnp.broadcast_to(row, (n, n)), 0), axis=1, keepdims=True)


def split_heads(mixes, totals, step, keep_ref, msg_ref):
    upper = is_upper("head", step)
    for s, (mix, total) in enumerate(zip(mixes, totals)):
        half = mix.shape[0] // 2
        keep_ref[s, :, :HD] = jnp.where(upper, mix[half:], mix[:half])
        keep_ref[s, :, HD:] = jnp.where(upper, total[half:], total[:half])
        send = jnp.where(upper, total[:half], total[half:])
        rough = send.astype(BF16)
        msg_ref[s, :, :HD] = jnp.where(upper, mix[:half], mix[half:]).astype(BF16)
        msg_ref[s, :, HD : 2 * HD] = rough
        msg_ref[s, :, 2 * HD :] = (send - rough.astype(F32)).astype(BF16)


def attend(every, slot_row, length_row, cache_key, cache_value, widths, step):
    slots, span, nk = cache_key.shape
    nq = widths[0]
    kv, heads = nk // HD, nq // HD
    group = heads // kv
    scale = 1.0 / math.sqrt(HD)

    def body(every_ref, slot_ref, length_ref, key_ref, value_ref, keep_ref, msg_ref):
        head_place = lax.axis_index("head")
        slot_col = to_column(slot_ref[...])
        length_col = to_column(length_ref[...])
        rows = every_ref[...].astype(F32)
        mixes, totals = [], []
        for s in range(slots):
            chosen = slot_col == lax.axis_index("pool") * slots + s
            row = jnp.sum(jnp.where(chosen, rows, 0.0), axis=0, keepdims=True)
            length = jnp.sum(jnp.where(chosen, length_col, 0), axis=0, keepdims=True)
            stacked = []
            for k in range(kv):
                at = k * group * HD
                piece = jnp.concatenate(
                    [row[:, at + g * HD : at + (g + 1) * HD] for g in range(group)], 0
                )
                stacked.append(piece)
            queries = jnp.concatenate(stacked, 0)
            wide = []
            for k in range(kv):
                blank = jnp.zeros((group, HD), F32)
                wide.append(jnp.concatenate([stacked[k] if c == k else blank for c in range(kv)], 1))
            wide = jnp.concatenate(wide, 0).astype(BF16)
            scores = scale * lax.dot_general(
                wide, key_ref[s], (((1,), (1,)), ((), ())), preferred_element_type=F32
            )
            position = head_place * span + lax.broadcasted_iota(jnp.int32, (heads, span), 1)
            weights = jnp.where(position < length, jnp.exp(scores), 0.0)
            total = jnp.sum(weights, axis=1, keepdims=True)
            full = jnp.dot(weights.astype(BF16), value_ref[s], preferred_element_type=F32)
            mix = jnp.concatenate(
                [full[k * group : (k + 1) * group, k * HD : (k + 1) * HD] for k in range(kv)], 0
            )

            def spread(offset):
                return jnp.concatenate(
                    [
                        jnp.broadcast_to(row[:, offset + k * HD : offset + (k + 1) * HD], (group, HD))
                        for k in range(kv)
                    ],
                    0,
                )

            own = jnp.exp(jnp.sum(queries * spread(nq), axis=1, keepdims=True) * scale)
            own = jnp.where(head_place == 0, own, 0.0)
            mixes.append(mix + own * spread(nq + nk))
            totals.append(jnp.broadcast_to(total + own, (heads, HD)))
        split_heads(mixes, totals, step, keep_ref, msg_ref)

    return call(
        body,
        (
            shaped((slots, heads // 2, 2 * HD), F32),
            shaped((slots, heads // 2, 3 * HD), BF16),
        ),
        [VM] * 5,
        grant=4 * MIB,
    )(every, slot_row, length_row, cache_key, cache_value)


def add_part(keep_ref, came_ref, s):
    came = came_ref[s].astype(F32)
    mix = keep_ref[s, :, :HD] + came[:, :HD]
    total = keep_ref[s, :, HD:] + came[:, HD : 2 * HD] + came[:, 2 * HD :]
    return mix, total


def split_again(keep, came, step):
    slots, heads = keep.shape[:2]

    def body(keep_in, came_ref, keep_ref, msg_ref):
        mixes, totals = zip(*[add_part(keep_in, came_ref, s) for s in range(slots)])
        split_heads(mixes, totals, step, keep_ref, msg_ref)

    return call(
        body,
        (shaped((slots, heads // 2, 2 * HD), F32), shaped((slots, heads // 2, 3 * HD), BF16)),
        [VM, VM],
    )(keep, came)


def finish(keep, came, gain_row):
    slots, heads = keep.shape[:2]
    chunk = gain_row.shape[1]

    def body(keep_ref, came_ref, gain_ref, msg_ref):
        rows = []
        for s in range(slots):
            mix, total = add_part(keep_ref, came_ref, s)
            out = mix / total
            rows.append(jnp.concatenate([out[j : j + 1, :] for j in range(heads)], 1))
        msg_ref[:, : heads * HD] = jnp.concatenate(rows, 0).astype(BF16)
        msg_ref[:, heads * HD :] = jnp.broadcast_to(gain_ref[...], (slots, chunk)).astype(BF16)

    return call(body, shaped((slots, heads * HD + chunk), BF16), [VM] * 3)(keep, came, gain_row)


def project(every, slot_row, weight, hidden, n_aux):
    depth, width = weight.shape
    requests, chunk = hidden.shape
    extra = every.shape[1] - depth

    def body(every_ref, slot_ref, w_ref, hid_ref, term_ref, msg_ref):
        place = lax.axis_index("head") * n_aux + lax.axis_index("aux")
        rows = every_ref[:, :depth].astype(F32)
        slot_col = to_column(slot_ref[...])
        sel = jnp.zeros((requests, depth), F32)
        for e in range(requests):
            sel = sel + jnp.where(slot_col == e, rows[e : e + 1, :], 0.0)
        term = jnp.dot(sel.astype(BF16), w_ref[...], preferred_element_type=F32)
        tiled = jnp.concatenate([hid_ref[...].astype(F32)] * (width // chunk), 1)
        owner = lax.broadcasted_iota(jnp.int32, term.shape, 1) // chunk == place
        term = term + jnp.where(owner, tiled, 0.0)
        term_ref[...] = term
        msg_ref[:, :width] = term.astype(BF16)
        msg_ref[:, width:] = every_ref[:, depth:]

    return call(
        body,
        (shaped((requests, width), F32), shaped((requests, width + extra), BF16)),
        [VM] * 4,
        grant=3 * MIB,
        cost=pl.CostEstimate(
            flops=2 * requests * weight.size, bytes_accessed=weight.size * 2, transcendentals=0
        ),
    )(every, slot_row, weight, hidden)


def add_terms(term, message, came, axis, step, last):
    requests, width = term.shape
    extra = message.shape[1] - width

    def body(term_ref, mine_ref, came_ref, *outs):
        upper = is_upper(axis, step)
        total = term_ref[...] + came_ref[:, :width].astype(F32)
        a, b = mine_ref[:, width:], came_ref[:, width:]
        low, high = jnp.where(upper, b, a), jnp.where(upper, a, b)
        if last:
            outs[0][...] = total.astype(BF16)
            outs[1][:, :extra] = low
            outs[1][:, extra:] = high
        else:
            outs[0][...] = total
            outs[1][:, :width] = total.astype(BF16)
            outs[1][:, width : width + extra] = low
            outs[1][:, width + extra :] = high

    if last:
        outs = (shaped((requests, width), BF16), shaped((requests, 2 * extra), BF16))
    else:
        outs = (shaped((requests, width), F32), shaped((requests, width + 2 * extra), BF16))
    return call(body, outs, [VM] * 3)(term, message, came)


def score(stream, gains, resident, lm_head):
    requests, depth = stream.shape
    width = lm_head.shape[1]
    block = gains.shape[1]
    held = len(resident)
    rows = depth // PIECES
    start = held * rows
    left = PIECES - held
    slots = min(3, left)
    stride = gains.shape[0] // (depth // block)

    def body(stream_ref, gain_ref, *refs):
        kept = refs[:held]
        src, out_ref, sum_ref, x_ref, buf, sem = refs[held:]

        def copy(i):
            return pltpu.make_async_copy(
                src.at[pl.ds(start + i * rows, rows)], buf.at[i % slots], sem.at[i % slots]
            )

        for i in range(slots):
            copy(i).start()
        squares = jnp.zeros((requests, 1), F32)
        for p in range(depth // block):
            part = stream_ref[:, p * block : (p + 1) * block].astype(F32)
            squares = squares + jnp.sum(part * part, axis=1, keepdims=True)
        factor = lax.rsqrt(squares / depth + 1e-05)
        for p in range(depth // block):
            part = stream_ref[:, p * block : (p + 1) * block].astype(F32)
            gain = gain_ref[p * stride : p * stride + 1, :].astype(F32)
            x_ref[:, p * block : (p + 1) * block] = (part * factor * gain).astype(BF16)

        def multiply(ref, piece, first=False):
            part = jnp.dot(
                x_ref[:, piece * rows : (piece + 1) * rows], ref[...], preferred_element_type=F32
            )
            out_ref[...] = part if first else out_ref[...] + part

        done = 0
        for i in range(held):
            multiply(kept[i], i, i == 0)
            while done < left and done * held < (i + 1) * left:
                copy(done).wait()
                multiply(buf.at[done % slots], held + done)
                if done + slots < left:
                    copy(done + slots).start()
                done += 1
        logits = out_ref[...]
        expd = jnp.exp(logits)
        total = jnp.sum(expd, axis=1, keepdims=True)
        moment = jnp.sum(expd * logits, axis=1, keepdims=True)
        lane = lax.broadcasted_iota(jnp.int32, (requests, 128), 1)
        sum_ref[...] = jnp.where(lane == 0, total, moment)

    return call(
        body,
        (shaped((requests, width), F32), shaped((requests, 128), F32)),
        [VM] * (2 + held) + [HB],
        [
            pltpu.VMEM((requests, depth), BF16),
            pltpu.VMEM((slots, rows, width), BF16),
            pltpu.SemaphoreType.DMA((slots,)),
        ],
        slots * rows * width * 2 + 4 * MIB,
        pl.CostEstimate(
            flops=2 * requests * lm_head.size,
            bytes_accessed=left * rows * width * 2,
            transcendentals=requests * width,
        ),
    )(stream, gains, *resident, lm_head)


def make_per_device(sizes):
    n_pool, n_head, n_aux = sizes["pool"], sizes["head"], sizes["aux"]

    def per_device(
        hidden,
        gain,
        queries,
        new_key,
        new_value,
        cache_key,
        cache_value,
        lengths,
        slot_of,
        out_proj,
        lm_head,
    ):
        rounds = Rounds(lm_head)
        slot_row, length_row = slot_of.reshape(1, -1), lengths.reshape(1, -1)

        every = gather(rounds, join(queries, new_key, new_value), "pool", n_pool, 0)

        widths = (queries.shape[1], new_key.shape[1])
        halves = steps_of(n_head)[::-1]
        keep, message = attend(
            every, slot_row, length_row, cache_key, cache_value, widths, halves[0]
        )
        for i, step in enumerate(halves):
            came = rounds.swap(message, "head", n_head, step)
            if i + 1 < len(halves):
                keep, message = split_again(keep, came, halves[i + 1])
        message = finish(keep, came, gain.reshape(1, -1))
        every = gather(rounds, message, "pool", n_pool, 0)

        term, message = project(every, slot_row, out_proj[0], hidden, n_aux)
        todo = [("aux", n_aux, s) for s in steps_of(n_aux)]
        todo += [("head", n_head, s) for s in steps_of(n_head)]
        for i, (axis, size, step) in enumerate(todo):
            came = rounds.swap(message, axis, size, step)
            term, message = add_terms(term, message, came, axis, step, i + 1 == len(todo))

        stream = gather(rounds, term, "pool", n_pool, 1)
        logits, sums = score(stream, message, rounds.resident, lm_head)
        for axis, size in (("aux", n_aux), ("head", n_head), ("pool", n_pool)):
            for step in steps_of(size):
                sums = sums + rounds.swap(sums, axis, size, step)
        entropy = jnp.log(sums[:, 0]) - sums[:, 1] / sums[:, 0]
        return (logits, entropy)

    return per_device


def solution(mesh):
    in_specs = (
        P("grp", ("pool", "head", "aux")),
        P(("pool", "head", "aux")),
        P(("grp", "pool"), "aux"),
        P(("grp", "pool"), "aux"),
        P(("grp", "pool"), "aux"),
        P(("grp", "pool"), "head", "aux"),
        P(("grp", "pool"), "head", "aux"),
        P("grp"),
        P("grp"),
        P("aux", "head", "pool"),
        P(None, ("pool", "head", "aux")),
    )
    out_specs = (P("grp", ("pool", "head", "aux")), P("grp"))
    return jax.shard_map(
        make_per_device(dict(mesh.shape)),
        mesh=mesh,
        in_specs=in_specs,
        out_specs=out_specs,
        check_vma=False,
    )
```
